32 devices in a mesh: dp: 8 (over y, x, core), pencil: 4 (over z).
Axes of the slice: x: 2, y: 2, z: 4, core: 2. Of those that a mesh axis runs over, the one named last changes fastest.
Arguments:
- field: bfloat16 [8, 64, 64, 64, 128], P('dp', 'pencil'), may hold values from -6 to 6
- cotangent: bfloat16 [8, 64, 64, 64, 128], P('dp', 'pencil'), may hold values from -6 to 6
- w_spec: bfloat16 [16, 16, 16, 64, 128], P('dp', 'pencil'), may hold values from -6 to 6
- w_local: bfloat16 [64, 64], replicated, may hold values from -0.75 to 0.75
Outputs:
- grad_field: bfloat16 [8, 64, 64, 64, 128], P('dp', 'pencil')
- grad_w: float32 [16, 16, 16, 64, 128], P('dp', 'pencil')
The draws below stay inside these ranges and needn't reach their ends.
All inputs are finite; a program needn't handle non-finite values.
Results may differ from the reference program's by a relative error of at most 0.02.
Values may be sent and summed in bfloat16 or wider, within the bound.
A program may use at most 192 MiB of HBM per device.

```python
import math
import jax
import jax.numpy as jnp
from jax import lax

NX = 64
NY = 64
NZ = 128
CH = 64
MX = 16
MY = 16
MZ = 16
SAMPLES = 8


def block_levels(stream_key, shape, shards, smallest, largest):
    def one(dim, parts):
        draws = jax.random.uniform(jax.random.fold_in(jax.random.fold_in(stream_key, 6), dim), (parts,), jnp.float32, smallest / len(shards), largest / len(shards))
        return jnp.repeat(jnp.exp(draws), shape[dim] // parts).reshape((-1,) + (1,) * (len(shape) - dim - 1))

    level = one(*shards[0])
    for cut in shards[1:]:
        level = level * one(*cut)
    return level


def bell_draw(own_key, shape, scale, bound, cuts=(), kind=jnp.bfloat16):
    entries = jax.random.normal(own_key, shape, jnp.float32) * scale
    if len(cuts) > 0:
        entries = block_levels(own_key, shape, cuts, -0.22, 0.18) * entries
    return jnp.clip(entries, min=-bound, max=bound).astype(kind)


def setup_inputs(seed: int = 0) -> dict:
    arg_keys = jax.random.split(jax.random.key(seed), 5)
    field = bell_draw(arg_keys[0], (SAMPLES, NX, NY, CH, NZ), 1.0, 6.0, ((0, 8), (1, 4)))
    cotangent = bell_draw(arg_keys[1], (SAMPLES, NX, NY, CH, NZ), 1.0, 6.0, ((0, 8), (1, 4)))
    w_spec = bell_draw(arg_keys[2], (MX, MY, MZ, CH, 2 * CH), 1.0, 6.0, ((0, 8), (1, 4)))
    w_local = bell_draw(arg_keys[3], (CH, CH), CH ** -0.5, 0.75)
    return {"field": field, "cotangent": cotangent, "w_spec": w_spec, "w_local": w_local}


HIGHEST = lax.Precision.HIGHEST

def phase_pair(length, mode_count, signed):
    position = jnp.arange(length, dtype=jnp.int32)
    indices = jnp.arange(mode_count, dtype=jnp.int32)
    frequency = jnp.where(indices < mode_count // 2, indices, indices - mode_count) if signed else indices
    product = jnp.mod(position[:, None] * frequency[None, :], length).astype(jnp.float32)
    angles = product * (2.0 * math.pi / length)
    return (jnp.cos(angles), jnp.sin(angles))

def grid_tables():
    cos_x, sin_x = phase_pair(NX, MX, True)
    cos_y, sin_y = phase_pair(NY, MY, True)
    cos_z, sin_z = phase_pair(NZ, MZ, False)
    forward_z = jnp.concatenate([cos_z, -sin_z], 1).astype(jnp.bfloat16)
    weight_z = jnp.where(jnp.arange(MZ, dtype=jnp.int32) == 0, 1.0, 2.0).astype(jnp.float32) / (NX * NY * NZ)
    inverse_z = jnp.concatenate([cos_z * weight_z, -sin_z * weight_z], 1).T
    adjoint_z = jnp.concatenate([cos_z, -sin_z], 1).T
    spectrum_scale = jnp.concatenate([weight_z, weight_z])
    return (cos_x, sin_x, cos_y, sin_y, forward_z, inverse_z, adjoint_z, spectrum_scale)

def rotate_half(values):
    middle = values.shape[-1] // 2
    return jnp.concatenate([values[..., middle:], -values[..., :middle]], -1)

def along_y(values, cosines, sine_table, inverse):
    pattern = 'xjck,yj->xyck' if inverse else 'xyck,yj->xjck'
    factor = -1.0 if inverse else 1.0
    direct = jnp.einsum(pattern, values, cosines, precision=HIGHEST)
    turned = jnp.einsum(pattern, rotate_half(values), sine_table, precision=HIGHEST)
    return direct + factor * turned

def along_x(values, cosines, sine_table, inverse):
    pattern = 'jbck,xj->xbck' if inverse else 'xbck,xj->jbck'
    factor = -1.0 if inverse else 1.0
    direct = jnp.einsum(pattern, values, cosines, precision=HIGHEST)
    turned = jnp.einsum(pattern, rotate_half(values), sine_table, precision=HIGHEST)
    return direct + factor * turned

def z_forward(field_in, matrix):
    shape_in = field_in.shape
    product = jnp.dot(field_in.reshape(-1, shape_in[-1]), matrix, preferred_element_type=jnp.float32)
    return product.reshape(shape_in[:-1] + (matrix.shape[1],))

def z_back(values, matrix):
    shape_in = values.shape
    product = jnp.dot(values.reshape(-1, shape_in[-1]), matrix, precision=HIGHEST, preferred_element_type=jnp.float32)
    return product.reshape(shape_in[:-1] + (matrix.shape[1],))

def gelu_slope(pre):
    normal_cdf = 0.5 * (1.0 + lax.erf(pre * (1.0 / math.sqrt(2.0))))
    return normal_cdf + pre * jnp.exp(-0.5 * pre * pre) * (1.0 / math.sqrt(2.0 * math.pi))

def apply_modes(coeffs, weights):
    real_part = coeffs[..., :MZ]
    imag_part = coeffs[..., MZ:]
    from_real = jnp.einsum('abik,abkio->abok', real_part, weights, precision=HIGHEST)
    from_imag = jnp.einsum('abik,abkio->abok', imag_part, weights, precision=HIGHEST)
    out_real = from_real[:, :, :CH] - from_imag[:, :, CH:]
    out_imag = from_real[:, :, CH:] + from_imag[:, :, :CH]
    return jnp.concatenate([out_real, out_imag], -1)

def paired(g_modes):
    g_real = g_modes[..., :MZ]
    g_imag = g_modes[..., MZ:]
    return (jnp.concatenate([g_real, g_imag], -2), jnp.concatenate([g_imag, -g_real], -2))

def adjoint_modes(g_modes, weights):
    paired_one, paired_two = paired(g_modes)
    back_real = jnp.einsum('abkio,abok->abik', weights, paired_one, precision=HIGHEST)
    back_imag = jnp.einsum('abkio,abok->abik', weights, paired_two, precision=HIGHEST)
    return jnp.concatenate([back_real, back_imag], -1)

def mode_grads(u_modes, g_modes):
    paired_one, paired_two = paired(g_modes)
    from_real = jnp.einsum('abik,abok->abkio', u_modes[..., :MZ], paired_one, precision=HIGHEST)
    from_imag = jnp.einsum('abik,abok->abkio', u_modes[..., MZ:], paired_two, precision=HIGHEST)
    return from_real + from_imag

def reference(field, cotangent, w_spec, w_local):
    cos_x, sin_x, cos_y, sin_y, forward_z, inverse_z, adjoint_z, spectrum_scale = grid_tables()
    w_full = w_spec.astype(jnp.float32)
    w_bypass = w_local.astype(jnp.float32)

    def to_modes(field_in):
        sectioned = along_y(z_forward(field_in, forward_z), cos_y, sin_y, False)
        return along_x(sectioned, cos_x, sin_x, False)

    def to_grid(coeffs, matrix):
        sectioned = along_y(along_x(coeffs, cos_x, sin_x, True), cos_y, sin_y, True)
        return z_back(sectioned, matrix)

    def one_sample(accumulated, pair_in):
        sample, target = pair_in
        u_modes = lax.optimization_barrier(to_modes(sample).astype(jnp.bfloat16)).astype(jnp.float32)
        v_modes = apply_modes(u_modes, w_full)
        values = to_grid(v_modes, inverse_z)
        bypass = jnp.einsum('xycz,co->xyoz', sample.astype(jnp.float32), w_bypass, precision=HIGHEST)
        slope_in = (target.astype(jnp.float32) * gelu_slope(values + bypass)).astype(jnp.bfloat16)
        g_modes = lax.optimization_barrier((to_modes(slope_in) * spectrum_scale).astype(jnp.bfloat16)).astype(jnp.float32)
        accumulated = accumulated + mode_grads(u_modes, g_modes)
        back_modes = adjoint_modes(g_modes, w_full)
        spread = jnp.einsum('xyoz,co->xycz', slope_in.astype(jnp.float32), w_bypass, precision=HIGHEST)
        grad_sample = (to_grid(back_modes, adjoint_z) + spread).astype(jnp.bfloat16)
        return (accumulated, grad_sample)
    initial = jnp.zeros((MX, MY, MZ, CH, 2 * CH), jnp.float32)
    grad_w, grad_field = lax.scan(one_sample, initial, (field, cotangent))
    return (grad_field, grad_w)
```

```python
import functools
import math

import jax
import jax.numpy as jnp
import numpy as np
from jax import lax
from jax.experimental import pallas as pl
from jax.experimental.pallas import tpu as pltpu
from jax.sharding import PartitionSpec as P

BF16 = jnp.bfloat16
F32 = jnp.float32
ROWS = 16
NXB = 2
YB = 4
VMEM = 64 * 1000 * 1024


def waves(length, count, signed):
    index = np.arange(count)
    freq = np.where(index < count // 2, index, index - count) if signed else index
    angle = 2.0 * math.pi * ((np.arange(length)[:, None] * freq[None, :]) % length) / length
    return np.cos(angle), np.sin(angle)


def kron_rows(matrix):
    return np.kron(matrix, np.eye(ROWS))


def const(array):
    return jnp.asarray(np.asarray(array, np.float32), BF16)


def make_tables(nx, ny, nz, groups, mx, my, mz, pencils):
    cx, sx = waves(nx, mx, True)
    cy, sy = waves(ny, my, True)
    cz, sz = waves(nz, mz, False)
    eye_g = np.eye(groups)
    plain = np.concatenate([cz, -sz], 1)
    turned = np.concatenate([-sz, -cz], 1)
    z_fwd = np.concatenate([np.kron(eye_g, plain), np.kron(eye_g, turned)], 1)
    weight = np.where(np.arange(mz) == 0, 1.0, 2.0) / (nx * ny * nz)
    z_inv = np.kron(eye_g, np.concatenate([cz * weight, -sz * weight], 1).T)
    z_adj = np.kron(eye_g, plain.T)
    half = np.eye(mz)
    zero = np.zeros((mz, mz))
    turn = np.kron(eye_g, np.block([[zero, -half], [half, zero]]))
    y_fwd = np.concatenate([kron_rows(cy.T), kron_rows(sy.T)], 1)
    y_inv = np.concatenate([kron_rows(cy), -kron_rows(sy)], 1)
    own = nx // pencils
    x_fwd, x_inv = [], []
    for q in range(pencils):
        c, s = cx[q * own : (q + 1) * own], sx[q * own : (q + 1) * own]
        x_fwd.append(np.concatenate([kron_rows(c.T), kron_rows(s.T)], 1))
        x_inv.append(np.concatenate([kron_rows(c), -kron_rows(s)], 1))
    scale = np.tile(np.concatenate([weight, weight]), groups)
    return dict(
        z_fwd=const(z_fwd),
        z_inv=const(z_inv),
        z_adj=const(z_adj),
        turn=const(turn),
        y_fwd=const(y_fwd),
        y_inv=const(y_inv),
        x_fwd=const(np.stack(x_fwd)),
        x_inv=const(np.stack(x_inv)),
        scale=jnp.asarray(scale, F32),
    )


def mm(a, b):
    return jnp.dot(a, b, preferred_element_type=F32)


def forward_zy(src, z_fwd, y_fwd, sections, step):
    nxb, ny, ch, nz = src.shape
    groups = ch // ROWS
    lanes = z_fwd.shape[1] // 2
    plain, turned = [], []
    for x in range(nxb):
        wide = jnp.concatenate(
            [src[x, :, g * ROWS : (g + 1) * ROWS, :].reshape(ny * ROWS, nz) for g in range(groups)], 1
        )
        spectral = mm(wide, z_fwd[...]).astype(BF16)
        plain.append(spectral[:, :lanes])
        turned.append(spectral[:, lanes:])
    stacked = jnp.concatenate([jnp.concatenate(plain, 1), jnp.concatenate(turned, 1)], 0)
    out = mm(y_fwd[...], stacked).astype(BF16)
    for x in range(nxb):
        sections[step * nxb + x] = out[:, x * lanes : (x + 1) * lanes]


def forward_x(sections, x_fwd, turn, out):
    pd, pp, jxl, jyl, _, lanes = out.shape
    xl = sections.shape[0]
    for p in range(pp):
        for b in range(jyl):
            j = p * jyl + b
            rows = sections[:, j * ROWS : (j + 1) * ROWS, :].reshape(xl * ROWS, lanes)
            both = jnp.concatenate([rows, mm(rows, turn[...]).astype(BF16)], 0)
            got = mm(x_fwd[...], both).astype(BF16)
            out[:, p, :, b] = got.reshape(pd, jxl, ROWS, lanes)


def inverse_x(modes, x_inv, turn, sections):
    pd, pp, jxl, jyl, _, lanes = modes.shape
    xl = sections.shape[0]
    for p in range(pp):
        for b in range(jyl):
            j = p * jyl + b
            rows = modes[:, p, :, b].reshape(pd * jxl * ROWS, lanes)
            both = jnp.concatenate([rows, mm(rows, turn[...]).astype(BF16)], 0)
            got = mm(x_inv[...], both).astype(BF16)
            sections[:, j * ROWS : (j + 1) * ROWS, :] = got.reshape(xl, ROWS, lanes)


def inverse_y(sections, turn, y_inv, columns, step, nxb):
    plain = [sections[step * nxb + x] for x in range(nxb)]
    turned = [mm(v, turn[...]).astype(BF16) for v in plain]
    stacked = jnp.concatenate([jnp.concatenate(plain, 1), jnp.concatenate(turned, 1)], 0)
    columns[...] = mm(y_inv[...], stacked).astype(BF16)


def inverse_z_mix(columns, z_inv, mix, src, emit):
    nxb, ny, ch, nz = src.shape
    groups = ch // ROWS
    lanes = z_inv.shape[0]

    def block(i, carry):
        y0 = pl.multiple_of(i * YB, YB)
        cols = columns[pl.ds(pl.multiple_of(i * (YB * ROWS), YB * ROWS), YB * ROWS), :]
        wide = jnp.concatenate([src[x, pl.ds(y0, YB)].reshape(YB * ch, nz) for x in range(nxb)], 1)
        mixed = mm(mix[...], wide)
        for x in range(nxb):
            grid = mm(cols[:, x * lanes : (x + 1) * lanes], z_inv[...]).reshape(YB, ROWS, groups * nz)
            grid = jnp.concatenate([grid[:, :, g * nz : (g + 1) * nz] for g in range(groups)], 1)
            emit(x, y0, grid + mixed[:, x * nz : (x + 1) * nz].reshape(YB, ch, nz))
        return carry

    lax.fori_loop(0, ny // YB, block, 0, unroll=2)


def gelu_slope(pre):
    normal_cdf = 0.5 * (1.0 + lax.erf(pre * (1.0 / math.sqrt(2.0))))
    return normal_cdf + pre * jnp.exp(-0.5 * pre * pre) * (1.0 / math.sqrt(2.0 * math.pi))


def first_kernel(field, z_fwd, y_fwd, x_fwd, turn, out, sections):
    step = pl.program_id(0)
    forward_zy(field, z_fwd, y_fwd, sections, step)

    @pl.when(step == pl.num_programs(0) - 1)
    def _():
        forward_x(sections, x_fwd, turn, out)


def middle_kernel(
    modes, field, target, mix, z_inv, y_inv, x_inv, z_fwd, y_fwd, x_fwd, turn,
    slope, out, sections_in, columns, sections_out,
):
    step = pl.program_id(0)

    @pl.when(step == 0)
    def _():
        inverse_x(modes, x_inv, turn, sections_in)

    inverse_y(sections_in, turn, y_inv, columns, step, field.shape[0])

    def emit(x, y0, pre):
        cot = target[x, pl.ds(y0, YB)].astype(F32)
        slope[x, pl.ds(y0, YB)] = (cot * gelu_slope(pre)).astype(BF16)

    inverse_z_mix(columns, z_inv, mix, field, emit)
    forward_zy(slope, z_fwd, y_fwd, sections_out, step)

    @pl.when(step == pl.num_programs(0) - 1)
    def _():
        forward_x(sections_out, x_fwd, turn, out)


def last_kernel(modes, slope, mix, z_adj, y_inv, x_inv, turn, grad, sections, columns):
    step = pl.program_id(0)

    @pl.when(step == 0)
    def _():
        inverse_x(modes, x_inv, turn, sections)

    inverse_y(sections, turn, y_inv, columns, step, slope.shape[0])

    def emit(x, y0, value):
        grad[x, pl.ds(y0, YB)] = value.astype(BF16)

    inverse_z_mix(columns, z_adj, mix, slope, emit)


def whole(array):
    return pl.BlockSpec(array.shape, lambda i, n=len(array.shape): (0,) * n)


def sliced(shape):
    return pl.BlockSpec((NXB,) + shape[1:], lambda i: (i, 0, 0, 0))


def params():
    return pltpu.CompilerParams(dimension_semantics=("arbitrary",), vmem_limit_bytes=VMEM)


def apply_kernel(u, w, v):
    half = u.shape[1] // 2
    ch = u.shape[2]
    for k in range(u.shape[0]):
        d = mm(u[k], w[k])
        real = d[:half, :ch] - d[half:, ch:]
        imag = d[:half, ch:] + d[half:, :ch]
        v[k] = jnp.concatenate([real, imag], 0)


def adjoint_kernel(u, g, w, grad_w, back):
    half = u.shape[1] // 2
    for k in range(u.shape[0]):
        gk = g[k]
        real, imag = gk[:half], gk[half:]
        pair = jnp.concatenate(
            [jnp.concatenate([real, imag], 1), jnp.concatenate([imag, -real], 1)], 0
        ).astype(BF16)
        back[k] = lax.dot_general(pair, w[k], (((1,), (1,)), ((), ())), preferred_element_type=F32)
        grad_w[k] = lax.dot_general(
            u[k], pair, (((0,), (0,)), ((), ())), preferred_element_type=F32
        )


def mode_call(kernel, mz, outs, *args):
    def spec(shape):
        return pl.BlockSpec((mz,) + shape[1:], lambda i: (i, 0, 0))

    return pl.pallas_call(
        kernel,
        grid=(args[0].shape[0] // mz,),
        in_specs=[spec(a.shape) for a in args],
        out_specs=[spec(o) for o in outs],
        out_shape=[jax.ShapeDtypeStruct(o, F32) for o in outs],
        compiler_params=params(),
    )(*args)


def solution(mesh):
    pd, pp = mesh.shape["dp"], mesh.shape["pencil"]
    axes = ("dp", "pencil")

    def body(field, cotangent, w_spec, w_local):
        sample, target = field[0], cotangent[0]
        xl, ny, ch, nz = sample.shape
        jxl, jyl, mz = w_spec.shape[:3]
        mx, my = jxl * pd, jyl * pp
        groups = ch // ROWS
        lanes = groups * 2 * mz
        t = make_tables(xl * pp, ny, nz, groups, mx, my, mz, pp)
        me = lax.axis_index("pencil")
        x_fwd = lax.dynamic_index_in_dim(t["x_fwd"], me, 0, keepdims=False)
        x_inv = lax.dynamic_index_in_dim(t["x_inv"], me, 0, keepdims=False)
        mix_eye = jnp.eye(YB, dtype=BF16)
        mix_in = jnp.kron(mix_eye, w_local.T)
        mix_out = jnp.kron(mix_eye, w_local)
        sent = jax.ShapeDtypeStruct((pd, pp, jxl, jyl, ROWS, lanes), BF16)
        grid_like = jax.ShapeDtypeStruct(sample.shape, BF16)
        sections = pltpu.VMEM((xl, my * ROWS, lanes), BF16)
        columns = pltpu.VMEM((ny * ROWS, NXB * lanes), BF16)
        steps = (xl // NXB,)

        def exchange(array):
            flat = array.reshape((pd * pp,) + array.shape[2:])
            return lax.all_to_all(flat, axes, split_axis=0, concat_axis=0, tiled=True)

        def gather_modes(parts):
            got = exchange(parts).reshape((pd, pp, jxl, jyl, ROWS, lanes))
            return got.astype(F32).sum(1)

        def per_mode(total):
            split = total.reshape(pd, jxl, jyl, ROWS, groups, 2, mz)
            turned = split.transpose(1, 2, 6, 5, 0, 4, 3)
            return turned.reshape(jxl * jyl * mz, 2 * pd, ch)

        def to_samples(modes):
            split = modes.astype(BF16).reshape(jxl, jyl, mz, 2, pd, groups, ROWS)
            turned = split.transpose(4, 0, 1, 6, 5, 3, 2).reshape(pd, 1, jxl, jyl, ROWS, lanes)
            out = jnp.broadcast_to(turned, (pd, pp) + turned.shape[2:])
            return exchange(out).reshape(sent.shape)

        weights = w_spec.reshape(jxl * jyl * mz, ch, 2 * ch)
        ins = (sample, t["z_fwd"], t["y_fwd"], x_fwd, t["turn"])
        u_parts = pl.pallas_call(
            first_kernel,
            grid=steps,
            in_specs=[sliced(sample.shape)] + [whole(a) for a in ins[1:]],
            out_specs=whole(sent),
            out_shape=sent,
            scratch_shapes=[sections],
            compiler_params=params(),
        )(*ins)
        u_modes = per_mode(gather_modes(u_parts)).astype(BF16)
        (v_modes,) = mode_call(apply_kernel, mz, [u_modes.shape], u_modes, weights)
        ins = (
            to_samples(v_modes), sample, target, mix_in, t["z_inv"], t["y_inv"], x_inv,
            t["z_fwd"], t["y_fwd"], x_fwd, t["turn"],
        )
        slope, g_parts = pl.pallas_call(
            middle_kernel,
            grid=steps,
            in_specs=[whole(ins[0]), sliced(sample.shape), sliced(sample.shape)]
            + [whole(a) for a in ins[3:]],
            out_specs=[sliced(sample.shape), whole(sent)],
            out_shape=[grid_like, sent],
            scratch_shapes=[sections, columns, sections],
            compiler_params=params(),
        )(*ins)
        g_modes = per_mode(gather_modes(g_parts) * t["scale"]).astype(BF16).astype(F32)
        grad_w, back = mode_call(
            adjoint_kernel, mz, [weights.shape, u_modes.shape], u_modes, g_modes, weights
        )
        ins = (to_samples(back), slope, mix_out, t["z_adj"], t["y_inv"], x_inv, t["turn"])
        grad = pl.pallas_call(
            last_kernel,
            grid=steps,
            in_specs=[whole(ins[0]), sliced(sample.shape)] + [whole(a) for a in ins[2:]],
            out_specs=sliced(sample.shape),
            out_shape=grid_like,
            scratch_shapes=[sections, columns],
            compiler_params=params(),
        )(*ins)
        return grad[None], grad_w.reshape(w_spec.shape)

    grid_spec = P("dp", "pencil", None, None, None)
    return jax.shard_map(
        body,
        mesh=mesh,
        in_specs=(grid_spec, grid_spec, grid_spec, P()),
        out_specs=(grid_spec, grid_spec),
        check_vma=False,
    )
```

```python
import functools
import math

import jax
import jax.numpy as jnp
import numpy as np
from jax import lax
from jax.experimental import pallas as pl
from jax.experimental.pallas import tpu as pltpu
from jax.sharding import PartitionSpec as P

BF16 = jnp.bfloat16
F32 = jnp.float32
ROWS = 16
NXB = 2
YB = 4
VMEM = 64 * 1000 * 1024


def waves(length, count, signed):
    index = np.arange(count)
    freq = np.where(index < count // 2, index, index - count) if signed else index
    angle = 2.0 * math.pi * ((np.arange(length)[:, None] * freq[None, :]) % length) / length
    return np.cos(angle), np.sin(angle)


def kron_rows(matrix):
    return np.kron(matrix, np.eye(ROWS))


def const(array):
    return jnp.asarray(np.asarray(array, np.float32), BF16)


def make_tables(nx, ny, nz, groups, mx, my, mz, pencils):
    cx, sx = waves(nx, mx, True)
    cy, sy = waves(ny, my, True)
    cz, sz = waves(nz, mz, False)
    eye_g = np.eye(groups)
    plain = np.concatenate([cz, -sz], 1)
    turned = np.concatenate([-sz, -cz], 1)
    z_fwd = np.concatenate([np.kron(eye_g, plain), np.kron(eye_g, turned)], 1)
    weight = np.where(np.arange(mz) == 0, 1.0, 2.0) / (nx * ny * nz)
    z_inv = np.kron(eye_g, np.concatenate([cz * weight, -sz * weight], 1).T)
    z_adj = np.kron(eye_g, plain.T)
    half = np.eye(mz)
    zero = np.zeros((mz, mz))
    turn = np.kron(eye_g, np.block([[zero, -half], [half, zero]]))
    y_fwd = np.concatenate([kron_rows(cy.T), kron_rows(sy.T)], 1)
    y_inv = np.concatenate([kron_rows(cy), -kron_rows(sy)], 1)
    own = nx // pencils
    x_fwd, x_inv = [], []
    for q in range(pencils):
        c, s = cx[q * own : (q + 1) * own], sx[q * own : (q + 1) * own]
        x_fwd.append(np.concatenate([kron_rows(c.T), kron_rows(s.T)], 1))
        x_inv.append(np.concatenate([kron_rows(c), -kron_rows(s)], 1))
    scale = np.tile(np.concatenate([weight, weight]), groups)
    return dict(
        z_fwd=const(z_fwd),
        z_inv=const(z_inv),
        z_adj=const(z_adj),
        turn=const(turn),
        y_fwd=const(y_fwd),
        y_inv=const(y_inv),
        x_fwd=const(np.stack(x_fwd)),
        x_inv=const(np.stack(x_inv)),
        scale=jnp.asarray(scale, F32),
    )


def mm(a, b):
    return jnp.dot(a, b, preferred_element_type=F32)


def forward_zy(src, z_fwd, y_fwd, sections, step):
    nxb, ny, ch, nz = src.shape
    groups = ch // ROWS
    lanes = z_fwd.shape[1] // 2
    plain, turned = [], []
    for x in range(nxb):
        wide = jnp.concatenate(
            [src[x, :, g * ROWS : (g + 1) * ROWS, :].reshape(ny * ROWS, nz) for g in range(groups)], 1
        )
        spectral = mm(wide, z_fwd[...]).astype(BF16)
        plain.append(spectral[:, :lanes])
        turned.append(spectral[:, lanes:])
    stacked = jnp.concatenate([jnp.concatenate(plain, 1), jnp.concatenate(turned, 1)], 0)
    out = mm(y_fwd[...], stacked).astype(BF16)
    for x in range(nxb):
        sections[step * nxb + x] = out[:, x * lanes : (x + 1) * lanes]


def forward_x(sections, x_fwd, turn, out):
    pd, pp, jxl, jyl, _, lanes = out.shape
    xl = sections.shape[0]
    for p in range(pp):
        for b in range(jyl):
            j = p * jyl + b
            rows = sections[:, j * ROWS : (j + 1) * ROWS, :].reshape(xl * ROWS, lanes)
            both = jnp.concatenate([rows, mm(rows, turn[...]).astype(BF16)], 0)
            got = mm(x_fwd[...], both).astype(BF16)
            out[:, p, :, b] = got.reshape(pd, jxl, ROWS, lanes)


def inverse_x(modes, x_inv, turn, sections):
    pd, pp, jxl, jyl, _, lanes = modes.shape
    xl = sections.shape[0]
    for p in range(pp):
        for b in range(jyl):
            j = p * jyl + b
            rows = modes[:, p, :, b].reshape(pd * jxl * ROWS, lanes)
            both = jnp.concatenate([rows, mm(rows, turn[...]).astype(BF16)], 0)
            got = mm(x_inv[...], both).astype(BF16)
            sections[:, j * ROWS : (j + 1) * ROWS, :] = got.reshape(xl, ROWS, lanes)


def inverse_y(sections, turn, y_inv, columns, step, nxb):
    plain = [sections[step * nxb + x] for x in range(nxb)]
    turned = [mm(v, turn[...]).astype(BF16) for v in plain]
    stacked = jnp.concatenate([jnp.concatenate(plain, 1), jnp.concatenate(turned, 1)], 0)
    columns[...] = mm(y_inv[...], stacked).astype(BF16)


def inverse_z_mix(columns, z_inv, mix, src, emit):
    nxb, ny, ch, nz = src.shape
    groups = ch // ROWS
    lanes = z_inv.shape[0]

    def block(i, carry):
        y0 = pl.multiple_of(i * YB, YB)
        cols = columns[pl.ds(pl.multiple_of(i * (YB * ROWS), YB * ROWS), YB * ROWS), :]
        wide = jnp.concatenate([src[x, pl.ds(y0, YB)].reshape(YB * ch, nz) for x in range(nxb)], 1)
        mixed = mm(mix[...], wide)
        for x in range(nxb):
            grid = mm(cols[:, x * lanes : (x + 1) * lanes], z_inv[...]).reshape(YB, ROWS, groups * nz)
            grid = jnp.concatenate([grid[:, :, g * nz : (g + 1) * nz] for g in range(groups)], 1)
            emit(x, y0, grid + mixed[:, x * nz : (x + 1) * nz].reshape(YB, ch, nz))
        return carry

    lax.fori_loop(0, ny // YB, block, 0, unroll=2)


def gelu_slope(pre):
    normal_cdf = 0.5 * (1.0 + lax.erf(pre * (1.0 / math.sqrt(2.0))))
    return normal_cdf + pre * jnp.exp(-0.5 * pre * pre) * (1.0 / math.sqrt(2.0 * math.pi))


def first_kernel(field, z_fwd, y_fwd, x_fwd, turn, out, sections):
    step = pl.program_id(0)
    forward_zy(field, z_fwd, y_fwd, sections, step)

    @pl.when(step == pl.num_programs(0) - 1)
    def _():
        forward_x(sections, x_fwd, turn, out)


def middle_kernel(
    modes, field, target, mix, z_inv, y_inv, x_inv, z_fwd, y_fwd, x_fwd, turn,
    slope, out, sections_in, columns, sections_out,
):
    step = pl.program_id(0)

    @pl.when(step == 0)
    def _():
        inverse_x(modes, x_inv, turn, sections_in)

    inverse_y(sections_in, turn, y_inv, columns, step, field.shape[0])

    def emit(x, y0, pre):
        cot = target[x, pl.ds(y0, YB)].astype(F32)
        slope[x, pl.ds(y0, YB)] = (cot * gelu_slope(pre)).astype(BF16)

    inverse_z_mix(columns, z_inv, mix, field, emit)
    forward_zy(slope, z_fwd, y_fwd, sections_out, step)

    @pl.when(step == pl.num_programs(0) - 1)
    def _():
        forward_x(sections_out, x_fwd, turn, out)


def last_kernel(modes, slope, mix, z_adj, y_inv, x_inv, turn, grad, sections, columns):
    step = pl.program_id(0)

    @pl.when(step == 0)
    def _():
        inverse_x(modes, x_inv, turn, sections)

    inverse_y(sections, turn, y_inv, columns, step, slope.shape[0])

    def emit(x, y0, value):
        grad[x, pl.ds(y0, YB)] = value.astype(BF16)

    inverse_z_mix(columns, z_adj, mix, slope, emit)


def whole(array):
    return pl.BlockSpec(array.shape, lambda i, n=len(array.shape): (0,) * n)


def sliced(shape):
    return pl.BlockSpec((NXB,) + shape[1:], lambda i: (i, 0, 0, 0))


def params():
    return pltpu.CompilerParams(dimension_semantics=("arbitrary",), vmem_limit_bytes=VMEM)


def load_modes(parts, scale, by_mode):
    pd, pp, _, rows, lanes = parts.shape
    total = parts[:, 0, 0].astype(F32)
    for q in range(1, pp):
        total = total + parts[:, q, 0].astype(F32)
    total = total * scale[...]
    turned = total.reshape(pd * rows, lanes).T
    count = by_mode.shape[0]
    for s in range(pd):
        own = turned[:, s * rows : (s + 1) * rows]
        pieces = [own[g * count : (g + 1) * count] for g in range(lanes // count)]
        by_mode[:, s, :] = jnp.concatenate(pieces, 1)


def store_modes(by_mode, out):
    pd, pp, _, rows, lanes = out.shape
    count = by_mode.shape[0]
    columns = []
    for s in range(pd):
        own = by_mode[:, s, :]
        pieces = [own[:, g * rows : (g + 1) * rows] for g in range(lanes // count)]
        columns.append(jnp.concatenate(pieces, 0))
    turned = jnp.concatenate(columns, 1).T.reshape(pd, rows, lanes).astype(BF16)
    for q in range(pp):
        out[:, q, 0] = turned


def apply_kernel(parts, w, scale, u, out, by_mode, result):
    load_modes(parts, scale, by_mode)
    mz, ch = w.shape[0], w.shape[1]
    half = by_mode.shape[1]
    for k in range(mz):
        uk = jnp.concatenate([by_mode[k], by_mode[mz + k]], 0).astype(BF16)
        u[k] = uk
        d = mm(uk, w[k])
        result[k] = d[:half, :ch] - d[half:, ch:]
        result[mz + k] = d[:half, ch:] + d[half:, :ch]
    store_modes(result, out)


def adjoint_kernel(parts, w, scale, u, grad_w, out, by_mode, result):
    load_modes(parts, scale, by_mode)
    mz = w.shape[0]
    half = by_mode.shape[1]
    for k in range(mz):
        real, imag = by_mode[k], by_mode[mz + k]
        pair = jnp.concatenate(
            [jnp.concatenate([real, imag], 1), jnp.concatenate([imag, -real], 1)], 0
        ).astype(BF16)
        back = lax.dot_general(pair, w[k], (((1,), (1,)), ((), ())), preferred_element_type=F32)
        result[k] = back[:half]
        result[mz + k] = back[half:]
        grad_w[k] = lax.dot_general(
            u[k], pair, (((0,), (0,)), ((), ())), preferred_element_type=F32
        )
    store_modes(result, out)


def mode_call(kernel, parts, w, scale, u):
    pd, pp, count, rows, lanes = parts.shape
    mz, ch = w.shape[0] // count, w.shape[1]
    first = u is None
    part_spec = pl.BlockSpec((pd, pp, 1, rows, lanes), lambda i: (0, 0, i, 0, 0))
    w_spec = pl.BlockSpec((mz,) + w.shape[1:], lambda i: (i, 0, 0))
    u_spec = pl.BlockSpec((mz, 2 * pd, ch), lambda i: (i, 0, 0))
    u_shape = jax.ShapeDtypeStruct((w.shape[0], 2 * pd, ch), BF16)
    w_shape = jax.ShapeDtypeStruct(w.shape, F32)
    by_mode = pltpu.VMEM((2 * mz, pd, ch), F32)
    return pl.pallas_call(
        kernel,
        grid=(count,),
        in_specs=[part_spec, w_spec, whole(scale)] + ([] if first else [u_spec]),
        out_specs=[u_spec if first else w_spec, part_spec],
        out_shape=[u_shape if first else w_shape, jax.ShapeDtypeStruct(parts.shape, BF16)],
        scratch_shapes=[by_mode, by_mode],
        compiler_params=params(),
    )(parts, w, scale, *(() if first else (u,)))


def solution(mesh):
    pd, pp = mesh.shape["dp"], mesh.shape["pencil"]
    axes = ("dp", "pencil")

    def body(field, cotangent, w_spec, w_local):
        sample, target = field[0], cotangent[0]
        xl, ny, ch, nz = sample.shape
        jxl, jyl, mz = w_spec.shape[:3]
        mx, my = jxl * pd, jyl * pp
        groups = ch // ROWS
        lanes = groups * 2 * mz
        t = make_tables(xl * pp, ny, nz, groups, mx, my, mz, pp)
        me = lax.axis_index("pencil")
        x_fwd = lax.dynamic_index_in_dim(t["x_fwd"], me, 0, keepdims=False)
        x_inv = lax.dynamic_index_in_dim(t["x_inv"], me, 0, keepdims=False)
        mix_eye = jnp.eye(YB, dtype=BF16)
        mix_in = jnp.kron(mix_eye, w_local.T)
        mix_out = jnp.kron(mix_eye, w_local)
        sent = jax.ShapeDtypeStruct((pd, pp, jxl, jyl, ROWS, lanes), BF16)
        grid_like = jax.ShapeDtypeStruct(sample.shape, BF16)
        sections = pltpu.VMEM((xl, my * ROWS, lanes), BF16)
        columns = pltpu.VMEM((ny * ROWS, NXB * lanes), BF16)
        steps = (xl // NXB,)

        def exchange(array):
            flat = array.reshape((pd * pp,) + array.shape[2:])
            got = lax.all_to_all(flat, axes, split_axis=0, concat_axis=0, tiled=True)
            return got.reshape(array.shape)

        def to_owner(parts):
            return exchange(parts).reshape((pd, pp, jxl * jyl, ROWS, lanes))

        def to_sample(modes):
            return exchange(modes).reshape(sent.shape)

        weights = w_spec.reshape(jxl * jyl * mz, ch, 2 * ch)
        ins = (sample, t["z_fwd"], t["y_fwd"], x_fwd, t["turn"])
        u_parts = pl.pallas_call(
            first_kernel,
            grid=steps,
            in_specs=[sliced(sample.shape)] + [whole(a) for a in ins[1:]],
            out_specs=whole(sent),
            out_shape=sent,
            scratch_shapes=[sections],
            compiler_params=params(),
        )(*ins)
        scale = t["scale"].reshape(1, 1, lanes)
        u_modes, v_modes = mode_call(
            apply_kernel, to_owner(u_parts), weights, jnp.ones_like(scale), None
        )
        ins = (
            to_sample(v_modes), sample, target, mix_in, t["z_inv"], t["y_inv"], x_inv,
            t["z_fwd"], t["y_fwd"], x_fwd, t["turn"],
        )
        slope, g_parts = pl.pallas_call(
            middle_kernel,
            grid=steps,
            in_specs=[whole(ins[0]), sliced(sample.shape), sliced(sample.shape)]
            + [whole(a) for a in ins[3:]],
            out_specs=[sliced(sample.shape), whole(sent)],
            out_shape=[grid_like, sent],
            scratch_shapes=[sections, columns, sections],
            compiler_params=params(),
        )(*ins)
        grad_w, back = mode_call(adjoint_kernel, to_owner(g_parts), weights, scale, u_modes)
        ins = (to_sample(back), slope, mix_out, t["z_adj"], t["y_inv"], x_inv, t["turn"])
        grad = pl.pallas_call(
            last_kernel,
            grid=steps,
            in_specs=[whole(ins[0]), sliced(sample.shape)] + [whole(a) for a in ins[2:]],
            out_specs=sliced(sample.shape),
            out_shape=grid_like,
            scratch_shapes=[sections, columns],
            compiler_params=params(),
        )(*ins)
        return grad[None], grad_w.reshape(w_spec.shape)

    grid_spec = P("dp", "pencil", None, None, None)
    return jax.shard_map(
        body,
        mesh=mesh,
        in_specs=(grid_spec, grid_spec, grid_spec, P()),
        out_specs=(grid_spec, grid_spec),
        check_vma=False,
    )
```
